1024 devices in a mesh: row: 64 (over y, x, core), col: 16 (over z).
Axes of the slice: x: 4, y: 8, z: 16, core: 2. Of those that a mesh axis runs over, the one named last changes fastest.
Arguments:
- weight: bfloat16 [8192, 24576], P('row', 'col'), may hold values from -6 to 6
- gradient: bfloat16 [8192, 24576], P('row', 'col'), may hold values from -80 to 80
- momentum: float32 [8192, 24576], P('row', 'col'), may hold values from -6 to 6
- old_basis: bfloat16 [256, 24576], P(None, 'col'), may hold values from -6 to 6
Outputs:
- new_weight: bfloat16 [8192, 24576], P('row', 'col')
- new_momentum: float32 [8192, 24576], P('row', 'col')
- new_basis: bfloat16 [256, 24576], P(None, 'col')
The draws below stay inside these ranges and needn't reach their ends.
All inputs are finite; a program needn't handle non-finite values.
Results may differ from the reference program's by a relative error of at most 0.0056.
Values may be sent and summed in bfloat16 or wider, within the bound.
A program may use at most 32 MiB of HBM per device.

```python
import math
import jax
import jax.numpy as jnp
from jax import lax

D = 8192
FF = 24576
RANK = 256


def draw_gradient(key, part):
    keys = jax.random.split(key, 2)
    base = jnp.clip(jax.random.normal(keys[0], (D, FF), jnp.float32), -6.0, 6.0)
    spread = jnp.exp(jax.random.uniform(keys[1], (FF,), jnp.float32, 0.0, math.log(10.0)))
    col_ramp = 1.0 + 2.0 * jnp.arange(FF, dtype=jnp.float32) / (FF - 1)
    row_ramp = 1.0 + 2.0 * jnp.arange(D, dtype=jnp.float32) / (D - 1)
    col_part = 0.1 * spread * col_ramp
    value = base * col_part[None, :] * row_ramp[:, None]
    return value.astype(jnp.bfloat16)


def shard_levels(key, dims, cuts, least, high):
    gain, own = 1.0, jax.random.fold_in(key, 6)
    for position, shards_of in cuts:
        steps = jnp.exp(jax.random.uniform(jax.random.fold_in(own, position), (shards_of,), jnp.float32, least / len(cuts), high / len(cuts)))
        gain = gain * jnp.repeat(steps, dims[position] // shards_of).reshape([-1 if axis == position else 1 for axis in range(len(dims))])
    return gain


def scatter_about(rng, shape, deviation, most, shards=(), kind=jnp.bfloat16):
    result = jax.random.normal(rng, shape, jnp.float32) * deviation
    if len(shards) > 0:
        result = shard_levels(rng, shape, shards, -0.22, 0.18) * result
    return jnp.clip(result, min=-most, max=most).astype(kind)


def setup_inputs(seed: int = 0) -> dict:
    splits = jax.random.split(jax.random.key(seed), 5)
    weight = scatter_about(splits[0], (D, FF), 1.0, 6.0, ((0, 64), (1, 16)))
    gradient = draw_gradient(jax.random.fold_in(splits[4], 71), 0)
    momentum = scatter_about(splits[2], (D, FF), 1.0, 6.0, ((0, 64), (1, 16)), jnp.float32)
    old_basis = scatter_about(splits[3], (RANK, FF), 1.0, 6.0, ((1, 16),))
    return dict(weight=weight, gradient=gradient, momentum=momentum, old_basis=old_basis)


epsilon = 1e-06
momentum_decay = 0.6
step_rate = 0.5

def reference(weight, gradient, momentum, old_basis):
    buffer = momentum + gradient.astype(jnp.float32)
    buffer_low = buffer.astype(jnp.bfloat16)
    left_factor = lax.dot_general(buffer_low.astype(jnp.float32), old_basis.astype(jnp.float32), (((1,), (1,)), ((), ())), preferred_element_type=jnp.float32)
    gram_matrix = lax.dot_general(left_factor.astype(jnp.float32), left_factor.astype(jnp.float32), (((0,), (0,)), ((), ())), precision=lax.Precision.HIGHEST, preferred_element_type=jnp.float32)
    chol_factor = jnp.linalg.cholesky(gram_matrix)
    orthonormal = lax.linalg.triangular_solve(chol_factor, left_factor, left_side=False, lower=True, transpose_a=True).astype(jnp.bfloat16)
    right_factor = lax.dot_general(orthonormal.astype(jnp.float32), buffer_low.astype(jnp.float32), (((0,), (0,)), ((), ())), preferred_element_type=jnp.float32)
    sum_squares = lax.optimization_barrier(jnp.sum(right_factor * right_factor, axis=1))
    col_scale = jnp.sqrt(sum_squares / FF + epsilon)
    new_basis = (right_factor / col_scale[:, None]).astype(jnp.bfloat16)
    scaled = (orthonormal.astype(jnp.float32) * col_scale[None, :]).astype(jnp.bfloat16)
    factor = step_rate * math.sqrt(D / RANK)

    def update_rows(row_blocks):
        buffer_rows, ortho_rows, scaled_rows, weight_rows = row_blocks
        correction = jnp.dot(scaled_rows.astype(jnp.float32), new_basis.astype(jnp.float32), preferred_element_type=jnp.float32)
        change = jnp.dot(ortho_rows.astype(jnp.float32), new_basis.astype(jnp.float32), preferred_element_type=jnp.float32)
        moved = buffer_rows - (1.0 - momentum_decay) * correction
        stepped = (weight_rows.astype(jnp.float32) - factor * change).astype(jnp.bfloat16)
        return (moved, stepped)
    blocks = 8
    shaped = tuple((part_rows.reshape(blocks, D // blocks, part_rows.shape[1]) for part_rows in (buffer, orthonormal, scaled, weight)))
    new_momentum, new_weight = lax.map(update_rows, shaped)
    return (new_weight.reshape(D, FF), new_momentum.reshape(D, FF), new_basis)
```

```python
import functools
import math

import jax
import jax.numpy as jnp
from jax import lax
from jax.experimental import pallas as pl
from jax.experimental.pallas import tpu as pltpu
from jax.sharding import PartitionSpec as P

epsilon = 1e-06
momentum_decay = 0.6
step_rate = 0.5

F32 = jnp.float32
BF16 = jnp.bfloat16
HI = lax.Precision.HIGHEST
MESH = pl.DeviceIdType.MESH
GROUP = 32


def tn(a, b):
    return lax.dot_general(a, b, (((0,), (0,)), ((), ())), precision=HI, preferred_element_type=F32)


def nt(a, b):
    return lax.dot_general(a, b, (((1,), (1,)), ((), ())), precision=HI, preferred_element_type=F32)


def spread(v, i):
    return jnp.broadcast_to(v[i : i + 1, :], (8, 128))


def fill(v, j):
    return jnp.broadcast_to(v[:, j : j + 1], (8, 128))


def small_inverse(p0):
    cols = [fill(p0, j) for j in range(8)]
    e = {(i, j): spread(cols[j], i) for j in range(8) for i in range(j, 8)}
    low, inv = {}, {}
    for j in range(8):
        r = lax.rsqrt(e[j, j])
        inv[j, j] = r
        for i in range(j + 1, 8):
            low[i, j] = e[i, j] * r
        for k in range(j + 1, 8):
            for i in range(k, 8):
                e[i, k] = e[i, k] - low[i, j] * low[k, j]
    for i in range(8):
        for j in range(i):
            s = low[i, j] * inv[j, j]
            for k in range(j + 1, i):
                s = s + low[i, k] * inv[k, j]
            inv[i, j] = -inv[i, i] * s
    return inv


def panel_step(t, panels, group):
    lane = lax.broadcasted_iota(jnp.int32, (8, 128), 1)
    sub = lax.broadcasted_iota(jnp.int32, (8, 128), 0)
    p = panels[0]
    p0, p1 = p[:, :128], p[:, 128:]
    inv = small_inverse(p0)
    a0 = jnp.where(lane < 8, (lane == sub).astype(F32), p0)
    q0, q1 = jnp.zeros((8, 128), F32), jnp.zeros((8, 128), F32)
    for j in range(8):
        col = jnp.zeros((8, 128), F32)
        for i in range(j, 8):
            col = jnp.where(sub == i, inv[i, j], col)
        q0 = q0 + col * spread(a0, j)
        q1 = q1 + col * spread(p1, j)
    r0 = [spread(q0, k) for k in range(8)]
    r1 = [spread(q1, k) for k in range(8)]
    out = []
    for s in range(1, group):
        b0, b1 = panels[s][:, :128], panels[s][:, 128:]
        live = t + s < group
        cols = [jnp.where(live, fill(b0, j), 0.0) for j in range(8)]
        b0 = jnp.where(jnp.logical_and(lane < 8, live), 0.0, b0)
        for k in range(8):
            m = cols[0] * inv[k, 0]
            for j in range(1, k + 1):
                m = m + cols[j] * inv[k, j]
            b0 = b0 - m * r0[k]
            b1 = b1 - m * r1[k]
        out.append(jnp.concatenate([b0, b1], axis=1))
    out.append(jnp.concatenate([q0, q1], axis=1))
    return tuple(pltpu.roll(v, 248, 1) for v in out)


def inverse_factor(work, size, rows, midway):
    group = rows // 8
    for ob in range(size // rows):
        lo = ob * rows
        if 2 * lo == size:
            midway()
        panels = tuple(work[lo + 8 * i : lo + 8 * i + 8, :] for i in range(group))
        panels = lax.fori_loop(0, group, lambda t, ps: panel_step(t, ps, group), panels)
        q = jnp.concatenate(panels, axis=0)
        rest = size - lo - rows
        lane = lax.broadcasted_iota(jnp.int32, (rows, size), 1)
        row = lax.broadcasted_iota(jnp.int32, (rows, size), 0)
        own = jnp.where(jnp.logical_or(lane < rest, lane > row + (size - rows)), 0.0, q)
        if ob:
            work[:lo, :] = pltpu.roll(work[:lo, :], size - rows, 1)
        work[lo : lo + rows, :] = own
        if rest:
            lane = lax.broadcasted_iota(jnp.int32, (rest, size), 1)
            old = jnp.where(lane < rows, 0.0, work[lo + rows :, :])
            both = jnp.where(lax.broadcasted_iota(jnp.int32, (rows, size), 1) < rest, q, own)
            work[lo + rows :, :] = pltpu.roll(old, size - rows, 1) - tn(q[:, :rest], both)


def far_first(k, n):
    h = (k + 1) // 2
    return n // 2 + h * (1 - 2 * (k % 2))


def take(ref, sem):
    pltpu.make_async_copy(ref, ref, sem).wait()


def exchange_kernel(
    sizes,
    gradient,
    momentum,
    basis,
    ortho_out,
    right_out,
    scale_out,
    grad_v,
    mom_v,
    basis_v,
    low,
    part,
    z_in,
    left,
    gram,
    gram_in,
    gram_own,
    gram_all,
    work,
    wide,
    core_in,
    core_sum,
    x_in,
    x_sum,
    y_in,
    right,
    square,
    square_z,
    square_own,
    square_r,
    load_sem,
    send_sem,
    recv_sem,
):
    ys, xs, zs, ff = sizes
    rows = ys * xs * 2
    half = ys * xs
    rank = 256
    r = lax.axis_index("row")
    c = lax.axis_index("col")
    core = lax.rem(r, 2)
    x = lax.rem(r // 2, xs)
    y = r // (2 * xs)
    owner = core * half + x * ys + y

    loads = [
        pltpu.make_async_copy(gradient, grad_v, load_sem.at[0]),
        pltpu.make_async_copy(momentum, mom_v, load_sem.at[1]),
        pltpu.make_async_copy(basis, basis_v, load_sem.at[2]),
    ]
    for copy in loads:
        copy.start()

    def send(src, dst, phase, row, col):
        pltpu.make_async_remote_copy(
            src_ref=src,
            dst_ref=dst,
            send_sem=send_sem.at[phase],
            recv_sem=recv_sem.at[phase],
            device_id=(row, col),
            device_id_type=MESH,
        ).start()

    def each_row(k, fn):
        d = far_first(k, rows)
        fn(d, lax.rem(r + d, rows))

    def each_col(k, fn):
        d = far_first(k, zs)
        fn(d, lax.rem(c + d, zs))

    def over_rows(fn):
        lax.fori_loop(0, rows - 1, lambda k, _: (each_row(k, fn), 0)[1], 0)

    def over_cols(fn):
        lax.fori_loop(0, zs - 1, lambda k, _: (each_col(k, fn), 0)[1], 0)

    barrier = pltpu.get_barrier_semaphore()
    over_cols(lambda d, p: pl.semaphore_signal(barrier, inc=1, device_id=(r, p), device_id_type=MESH))
    over_rows(lambda d, p: pl.semaphore_signal(barrier, inc=1, device_id=(p, c), device_id_type=MESH))

    for copy in loads:
        copy.wait()
    low[...] = (mom_v[...] + grad_v[...].astype(F32)).astype(BF16)
    local = lax.dot_general(
        low[...], basis_v[...], (((1,), (1,)), ((), ())), preferred_element_type=F32
    )
    part[...] = local.reshape(part.shape)
    pl.semaphore_wait(barrier, rows + zs - 2)

    over_cols(lambda d, p: send(part.at[p], z_in.at[d - 1], 0, r, p))
    mine = part[c]
    take(z_in, recv_sem.at[0])
    for k in range(zs - 1):
        mine = mine + z_in[k]
    left[c] = mine
    over_cols(lambda d, p: send(left.at[c], left.at[c], 1, r, p))
    take(z_in, recv_sem.at[1])

    left_rows = left[...].reshape(128, rank)
    whole = tn(left_rows, left_rows)
    each = 64 // rows
    for h in range(2):
        gram[h * 32 // each : (h + 1) * 32 // each] = whole[:, h * 128 : (h + 1) * 128].reshape(
            32 // each, each, 8, 128
        )
    over_rows(lambda d, p: send(gram.at[p], gram_in.at[d - 1], 2, p, c))

    high = left_rows.astype(BF16)
    rest = left_rows - high.astype(F32)
    middle = rest.astype(BF16)
    lowest = (rest - middle.astype(F32)).astype(BF16)
    count = rows // 4
    for q in range(4):
        cols = low[:, q * (ff // 4) : (q + 1) * (ff // 4)]
        block = sum(
            lax.dot_general(cols, t, (((0,), (0,)), ((), ())), preferred_element_type=F32)
            for t in (lowest, middle, high)
        )
        wide[q * count : (q + 1) * count] = block.reshape(count, ff // rows, rank)
    partner = r + 1 - 2 * core
    send(wide.at[pl.ds((1 - core) * half, half)], core_in, 3, partner, c)

    own = gram[r]
    take(gram_in, recv_sem.at[2])
    for k in range(rows - 1):
        own = own + gram_in[k]
    gram_own[...] = own
    gram_all[r] = own
    over_rows(lambda d, p: send(gram_own, gram_all.at[r], 4, p, c))

    take(core_in, recv_sem.at[3])
    core_sum[...] = core_in[...] + wide[pl.ds(core * half, half)]
    for d in range(1, xs):
        to = lax.rem(x + d, xs)
        send(core_sum.at[pl.ds(to * ys, ys)], x_in.at[d - 1], 5, (y * xs + to) * 2 + core, c)

    def middle_of_factor():
        take(x_in, recv_sem.at[5])
        total = core_sum[pl.ds(x * ys, ys)]
        for k in range(xs - 1):
            total = total + x_in[k]
        x_sum[...] = total

        def step(k, _):
            d = far_first(k, ys)
            to = lax.rem(y + d, ys)
            send(x_sum.at[to], y_in.at[d - 1], 6, (to * xs + x) * 2 + core, c)
            return 0

        lax.fori_loop(0, ys - 1, step, 0)

    take(gram_in, recv_sem.at[4])
    for h in range(2):
        work[:, h * 128 : (h + 1) * 128] = gram_all[h * 32 // each : (h + 1) * 32 // each].reshape(rank, 128)
    inverse_factor(work, rank, GROUP, middle_of_factor)

    take(y_in, recv_sem.at[6])
    slice_sum = x_sum[y]
    for k in range(ys - 1):
        slice_sum = slice_sum + y_in[k]
    inverse = work[...]
    mine = nt(slice_sum, inverse)
    right[owner] = mine.astype(BF16)
    square[...] = jnp.sum(mine * mine, axis=0, keepdims=True)
    over_cols(lambda d, p: send(square, square_z.at[d - 1], 7, r, p))

    def step(k, _):
        to = lax.rem(y + far_first(k, ys), ys)
        send(right.at[owner], right.at[owner], 8, (to * xs + x) * 2 + core, c)
        return 0

    lax.fori_loop(0, ys - 1, step, 0)

    ortho_out[...] = nt(left_rows, inverse).astype(BF16)

    take(square_z, recv_sem.at[7])
    total = square[...]
    for k in range(zs - 1):
        total = total + square_z[k]
    square_own[...] = total
    over_rows(lambda d, p: send(square_own, square_r.at[d - 1], 9, p, c))

    take(right.at[pl.ds(0, ys - 1)], recv_sem.at[8])
    block = pl.ds(core * half + x * ys, ys)
    for d in range(1, xs):
        to = lax.rem(x + d, xs)
        send(right.at[block], right.at[block], 10, (y * xs + to) * 2 + core, c)
    take(right.at[pl.ds(0, (xs - 1) * ys)], recv_sem.at[10])
    block = pl.ds(core * half, half)
    send(right.at[block], right.at[block], 11, partner, c)

    take(square_r, recv_sem.at[9])
    for k in range(rows - 1):
        total = total + square_r[k]
    scale_out[...] = jnp.sqrt(total / (ff * zs) + epsilon)
    take(right.at[pl.ds(0, half)], recv_sem.at[11])
    right_out[...] = right[...]

    take(z_in, send_sem.at[0])
    take(z_in, send_sem.at[1])
    take(gram_in, send_sem.at[2])
    take(core_in, send_sem.at[3])
    take(gram_in, send_sem.at[4])
    take(x_in, send_sem.at[5])
    take(y_in, send_sem.at[6])
    take(square_z, send_sem.at[7])
    take(right.at[pl.ds(0, ys - 1)], send_sem.at[8])
    take(square_r, send_sem.at[9])
    take(right.at[pl.ds(0, (xs - 1) * ys)], send_sem.at[10])
    take(right.at[pl.ds(0, half)], send_sem.at[11])


def finish_kernel(factor, weight, gradient, momentum, ortho, right, scale, weight_out, momentum_out, basis_out):
    cols = weight.shape[1]
    col_scale = scale[...]
    basis = right[...].astype(F32).reshape(cols, 256) / col_scale
    basis_low = basis.astype(BF16)
    basis_out[...] = basis_low.astype(F32).T.astype(BF16)
    rows = ortho[...]
    scaled = (rows.astype(F32) * col_scale).astype(BF16)
    dims = (((1,), (1,)), ((), ()))
    correction = lax.dot_general(scaled, basis_low, dims, preferred_element_type=F32)
    change = lax.dot_general(rows, basis_low, dims, preferred_element_type=F32)
    buffer = momentum[...] + gradient[...].astype(F32)
    momentum_out[...] = buffer - (1.0 - momentum_decay) * correction
    weight_out[...] = (weight[...].astype(F32) - factor * change).astype(BF16)


def per_device(sizes, dims, weight, gradient, momentum, old_basis):
    ys, xs, zs, ff = sizes
    rows, half, cut, lines = ys * xs * 2, ys * xs, ff // (ys * xs * 2), 128 // zs
    each = 64 // rows
    anywhere = pl.BlockSpec(memory_space=pl.ANY)
    inside = pl.BlockSpec(memory_space=pltpu.VMEM)
    ortho, right, scale = pl.pallas_call(
        functools.partial(exchange_kernel, sizes),
        out_shape=(
            jax.ShapeDtypeStruct((128, 256), BF16),
            jax.ShapeDtypeStruct((rows, cut, 256), BF16),
            jax.ShapeDtypeStruct((1, 256), F32),
        ),
        in_specs=[anywhere] * 3,
        out_specs=(inside, inside, inside),
        scratch_shapes=[
            pltpu.VMEM((128, ff), BF16),
            pltpu.VMEM((128, ff), F32),
            pltpu.VMEM((256, ff), BF16),
            pltpu.VMEM((128, ff), BF16),
            pltpu.VMEM((zs, lines, 256), F32),
            pltpu.VMEM((zs - 1, lines, 256), F32),
            pltpu.VMEM((zs, lines, 256), F32),
            pltpu.VMEM((rows, each, 8, 128), F32),
            pltpu.VMEM((rows - 1, each, 8, 128), F32),
            pltpu.VMEM((each, 8, 128), F32),
            pltpu.VMEM((rows, each, 8, 128), F32),
            pltpu.VMEM((256, 256), F32),
            pltpu.VMEM((rows, cut, 256), F32),
            pltpu.VMEM((half, cut, 256), F32),
            pltpu.VMEM((half, cut, 256), F32),
            pltpu.VMEM((xs - 1, ys, cut, 256), F32),
            pltpu.VMEM((ys, cut, 256), F32),
            pltpu.VMEM((ys - 1, cut, 256), F32),
            pltpu.VMEM((rows, cut, 256), BF16),
            pltpu.VMEM((1, 256), F32),
            pltpu.VMEM((zs - 1, 1, 256), F32),
            pltpu.VMEM((1, 256), F32),
            pltpu.VMEM((rows - 1, 1, 256), F32),
            pltpu.SemaphoreType.DMA((3,)),
            pltpu.SemaphoreType.DMA((12,)),
            pltpu.SemaphoreType.DMA((12,)),
        ],
        compiler_params=pltpu.CompilerParams(
            collective_id=0, has_side_effects=True, vmem_limit_bytes=40 * 1024 * 1024
        ),
    )(gradient, momentum, old_basis)
    total_rows, _ = dims
    factor = step_rate * math.sqrt(total_rows / 256)
    steps = 4
    wide = ff // steps
    strip = lambda n: pl.BlockSpec((n, wide), lambda i: (0, i))
    return pl.pallas_call(
        functools.partial(finish_kernel, factor),
        grid=(steps,),
        out_shape=(
            jax.ShapeDtypeStruct((128, ff), BF16),
            jax.ShapeDtypeStruct((128, ff), F32),
            jax.ShapeDtypeStruct((256, ff), BF16),
        ),
        in_specs=[
            strip(128),
            strip(128),
            strip(128),
            pl.BlockSpec((128, 256), lambda i: (0, 0)),
            pl.BlockSpec((rows // steps, cut, 256), lambda i: (i, 0, 0)),
            pl.BlockSpec((1, 256), lambda i: (0, 0)),
        ],
        out_specs=(strip(128), strip(128), strip(256)),
    )(weight, gradient, momentum, ortho, right, scale)


def solution(mesh, xs=4):
    rows, zs = mesh.shape["row"], mesh.shape["col"]
    sizes = (rows // (2 * xs), xs, zs, 1536)
    return jax.shard_map(
        functools.partial(per_device, sizes, (128 * rows, 1536 * zs)),
        mesh=mesh,
        in_specs=(P("row", "col"), P("row", "col"), P("row", "col"), P(None, "col")),
        out_specs=(P("row", "col"), P("row", "col"), P(None, "col")),
        check_vma=False,
    )
```

```python
import functools
import math

import jax
import jax.numpy as jnp
from jax import lax
from jax.experimental import pallas as pl
from jax.experimental.pallas import tpu as pltpu
from jax.sharding import PartitionSpec as P

epsilon = 1e-06
momentum_decay = 0.6
step_rate = 0.5

F32 = jnp.float32
BF16 = jnp.bfloat16
HI = lax.Precision.HIGHEST
MESH = pl.DeviceIdType.MESH
GROUP = 32
VMEM = 67043328


def nt(a, b):
    return lax.dot_general(a, b, (((1,), (1,)), ((), ())), precision=HI, preferred_element_type=F32)


def parts(a):
    high = a.astype(BF16)
    rest = a - high.astype(F32)
    middle = rest.astype(BF16)
    return high, middle, (rest - middle.astype(F32)).astype(BF16)


def tn6(a, b):
    ah, am, al = parts(a)
    bh, bm, bl = parts(b)
    left = jnp.concatenate([al, am, ah, am, ah, ah], axis=0)
    right = jnp.concatenate([bh, bm, bl, bh, bm, bh], axis=0)
    return lax.dot_general(left, right, (((0,), (0,)), ((), ())), preferred_element_type=F32)


def spread(v, i):
    return jnp.broadcast_to(v[i : i + 1, :], (8, 128))


def fill(v, j):
    return jnp.broadcast_to(v[:, j : j + 1], (8, 128))


def tree(terms):
    terms = list(terms)
    while len(terms) > 1:
        pairs = [a + b for a, b in zip(terms[::2], terms[1::2])]
        terms = pairs + terms[len(pairs) * 2 :]
    return terms[0]


def small_inverse(p0):
    cols = [fill(p0, j) for j in range(8)]
    e = {(i, j): spread(cols[j], i) for j in range(8) for i in range(j, 8)}
    low, inv = {}, {}
    for j in range(8):
        r = lax.rsqrt(e[j, j])
        inv[j, j] = r
        for i in range(j + 1, 8):
            low[i, j] = e[i, j] * r
        for k in range(j + 1, 8):
            for i in range(k, 8):
                e[i, k] = e[i, k] - low[i, j] * low[k, j]
    for i in range(8):
        for j in range(i):
            inv[i, j] = -inv[i, i] * tree(low[i, k] * inv[k, j] for k in range(j, i))
    return inv


def panel_step(t, panels, group):
    lane = lax.broadcasted_iota(jnp.int32, (8, 128), 1)
    sub = lax.broadcasted_iota(jnp.int32, (8, 128), 0)
    p = panels[0]
    p0, p1 = p[:, :128], p[:, 128:]
    inv = small_inverse(p0)
    a0 = jnp.where(lane < 8, (lane == sub).astype(F32), p0)
    columns = []
    for j in range(8):
        col = jnp.zeros((8, 128), F32)
        for i in range(j, 8):
            col = jnp.where(sub == i, inv[i, j], col)
        columns.append(col)
    q0 = tree(columns[j] * spread(a0, j) for j in range(8))
    q1 = tree(columns[j] * spread(p1, j) for j in range(8))
    r0 = [spread(q0, k) for k in range(8)]
    r1 = [spread(q1, k) for k in range(8)]
    out = []
    for s in range(1, group):
        b0, b1 = panels[s][:, :128], panels[s][:, 128:]
        live = t + s < group
        cols = [jnp.where(live, fill(b0, j), 0.0) for j in range(8)]
        b0 = jnp.where(jnp.logical_and(lane < 8, live), 0.0, b0)
        ms = [tree(cols[j] * inv[k, j] for j in range(k + 1)) for k in range(8)]
        b0 = b0 - tree(ms[k] * r0[k] for k in range(8))
        b1 = b1 - tree(ms[k] * r1[k] for k in range(8))
        out.append(jnp.concatenate([b0, b1], axis=1))
    out.append(jnp.concatenate([q0, q1], axis=1))
    return tuple(pltpu.roll(v, 248, 1) for v in out)


def inverse_factor(work, size, rows, midway):
    group = rows // 8
    for ob in range(size // rows):
        lo = ob * rows
        if 2 * lo == size:
            midway()
        panels = tuple(work[lo + 8 * i : lo + 8 * i + 8, :] for i in range(group))
        panels = lax.fori_loop(0, group, lambda t, ps: panel_step(t, ps, group), panels)
        q = jnp.concatenate(panels, axis=0)
        rest = size - lo - rows
        lane = lax.broadcasted_iota(jnp.int32, (rows, size), 1)
        row = lax.broadcasted_iota(jnp.int32, (rows, size), 0)
        own = jnp.where(jnp.logical_or(lane < rest, lane > row + (size - rows)), 0.0, q)
        if ob:
            work[:lo, :] = pltpu.roll(work[:lo, :], size - rows, 1)
        work[lo : lo + rows, :] = own
        if rest:
            lane = lax.broadcasted_iota(jnp.int32, (rest, size), 1)
            old = jnp.where(lane < rows, 0.0, work[lo + rows :, :])
            both = jnp.where(lax.broadcasted_iota(jnp.int32, (rows, size), 1) < rest, q, own)
            work[lo + rows :, :] = pltpu.roll(old, size - rows, 1) - tn6(q[:, :rest], both)
def far_first(k, n):
    h = (k + 1) // 2
    return n // 2 + h * (1 - 2 * (k % 2))


def take(ref, sem):
    pltpu.make_async_copy(ref, ref, sem).wait()


def exchange_kernel(
    sizes,
    gradient,
    momentum,
    basis,
    ortho_out,
    right_out,
    scale_out,
    grad_v,
    mom_v,
    basis_v,
    low,
    part,
    z_in,
    left,
    gram,
    gram_in,
    gram_own,
    gram_all,
    work,
    wide,
    core_in,
    core_sum,
    x_in,
    x_sum,
    y_in,
    right,
    square,
    square_z,
    square_own,
    square_r,
    square_half,
    square_core,
    gram_core,
    gram_pair,
    load_sem,
    send_sem,
    recv_sem,
):
    ys, xs, zs, ff = sizes
    rows = ys * xs * 2
    half = ys * xs
    rank = 256
    r = lax.axis_index("row")
    c = lax.axis_index("col")
    core = lax.rem(r, 2)
    x = lax.rem(r // 2, xs)
    y = r // (2 * xs)
    owner = core * half + x * ys + y
    chip = r // 2
    partner = r + 1 - 2 * core

    loads = [
        pltpu.make_async_copy(gradient, grad_v, load_sem.at[0]),
        pltpu.make_async_copy(momentum, mom_v, load_sem.at[1]),
        pltpu.make_async_copy(basis, basis_v, load_sem.at[2]),
    ]
    for copy in loads:
        copy.start()

    def drain(upto):
        sent = [
            z_in, z_in, gram_core, core_in, gram_in, x_in, y_in, square_z,
            right.at[pl.ds(0, ys - 1)], square_r.at[pl.ds(0, half - 1)],
            right.at[pl.ds(0, (xs - 1) * ys)], right.at[pl.ds(0, half)],
            gram_in, gram_core, square_core,
        ]
        for phase in range(upto):
            take(sent[phase], send_sem.at[phase])

    def send(src, dst, phase, row, col):
        pltpu.make_async_remote_copy(
            src_ref=src,
            dst_ref=dst,
            send_sem=send_sem.at[phase],
            recv_sem=recv_sem.at[phase],
            device_id=(row, col),
            device_id_type=MESH,
        ).start()

    def each_chip(k, fn):
        d = far_first(k, half)
        fn(d, 2 * lax.rem(chip + d, half) + core)

    def each_col(k, fn):
        d = far_first(k, zs)
        fn(d, lax.rem(c + d, zs))

    def over_chips(fn):
        lax.fori_loop(0, half - 1, lambda k, _: (each_chip(k, fn), 0)[1], 0)

    def over_cols(fn):
        lax.fori_loop(0, zs - 1, lambda k, _: (each_col(k, fn), 0)[1], 0)

    barrier = pltpu.get_barrier_semaphore()
    over_cols(lambda d, p: pl.semaphore_signal(barrier, inc=1, device_id=(r, p), device_id_type=MESH))
    over_chips(lambda d, p: pl.semaphore_signal(barrier, inc=1, device_id=(p, c), device_id_type=MESH))
    pl.semaphore_signal(barrier, inc=1, device_id=(partner, c), device_id_type=MESH)

    for copy in loads:
        copy.wait()
    low[...] = (mom_v[...] + grad_v[...].astype(F32)).astype(BF16)
    local = lax.dot_general(
        low[...], basis_v[...], (((1,), (1,)), ((), ())), preferred_element_type=F32
    )
    part[...] = local.reshape(part.shape)
    pl.semaphore_wait(barrier, half + zs - 1)

    over_cols(lambda d, p: send(part.at[p], z_in.at[d - 1], 0, r, p))
    mine = part[c]
    take(z_in, recv_sem.at[0])
    for k in range(zs - 1):
        mine = mine + z_in[k]
    left[c] = mine
    over_cols(lambda d, p: send(left.at[c], left.at[c], 1, r, p))
    take(z_in, recv_sem.at[1])

    left_rows = left[...].reshape(128, rank)
    whole = tn6(left_rows, left_rows)
    each = 32 // half
    for h in range(2):
        gram[h * half : (h + 1) * half] = whole[:, h * 128 : (h + 1) * 128].reshape(half, each, 8, 128)
    send(gram.at[pl.ds((1 - core) * half, half)], gram_core, 2, partner, c)

    take(gram_core, recv_sem.at[2])
    gram_pair[...] = gram_core[...] + gram[pl.ds(core * half, half)]
    over_chips(lambda d, p: send(gram_pair.at[p // 2], gram_in.at[d - 1], 12, p, c))

    high = left_rows.astype(BF16)
    rest = left_rows - high.astype(F32)
    middle = rest.astype(BF16)
    lowest = (rest - middle.astype(F32)).astype(BF16)
    count = rows // 4
    for q in range(4):
        cols = low[:, q * (ff // 4) : (q + 1) * (ff // 4)]
        block = sum(
            lax.dot_general(cols, t, (((0,), (0,)), ((), ())), preferred_element_type=F32)
            for t in (lowest, middle, high)
        )
        wide[q * count : (q + 1) * count] = block.reshape(count, ff // rows, rank)
    send(wide.at[pl.ds((1 - core) * half, half)], core_in, 3, partner, c)

    take(gram_in, recv_sem.at[12])
    own = gram_pair[chip]
    for k in range(half - 1):
        own = own + gram_in[k]
    gram_own[...] = own
    mine = core * half + chip
    gram_all[mine] = own
    over_chips(lambda d, p: send(gram_own, gram_all.at[mine], 4, p, c))

    take(core_in, recv_sem.at[3])
    core_sum[...] = core_in[...] + wide[pl.ds(core * half, half)]
    for d in range(1, xs):
        to = lax.rem(x + d, xs)
        send(core_sum.at[pl.ds(to * ys, ys)], x_in.at[d - 1], 5, (y * xs + to) * 2 + core, c)

    def middle_of_factor():
        take(x_in, recv_sem.at[5])
        total = core_sum[pl.ds(x * ys, ys)]
        for k in range(xs - 1):
            total = total + x_in[k]
        x_sum[...] = total

        def step(k, _):
            d = far_first(k, ys)
            to = lax.rem(y + d, ys)
            send(x_sum.at[to], y_in.at[d - 1], 6, (to * xs + x) * 2 + core, c)
            return 0

        lax.fori_loop(0, ys - 1, step, 0)

    take(gram_in, recv_sem.at[4])
    block = pl.ds(core * half, half)
    send(gram_all.at[block], gram_all.at[block], 13, partner, c)
    take(gram_core, recv_sem.at[13])
    for h in range(2):
        work[:, h * 128 : (h + 1) * 128] = gram_all[h * half : (h + 1) * half].reshape(rank, 128)
    inverse_factor(work, rank, GROUP, middle_of_factor)

    take(y_in, recv_sem.at[6])
    slice_sum = x_sum[y]
    for k in range(ys - 1):
        slice_sum = slice_sum + y_in[k]
    inverse = work[...]
    mine = nt(slice_sum, inverse)
    right[owner] = mine.astype(BF16)
    square[...] = jnp.sum(mine * mine, axis=0, keepdims=True)
    over_cols(lambda d, p: send(square, square_z.at[d - 1], 7, r, p))

    def step(k, _):
        to = lax.rem(y + far_first(k, ys), ys)
        send(right.at[owner], right.at[owner], 8, (to * xs + x) * 2 + core, c)
        return 0

    lax.fori_loop(0, ys - 1, step, 0)

    ortho_out[...] = nt(left_rows, inverse).astype(BF16)

    take(square_z, recv_sem.at[7])
    total = square[...]
    for k in range(zs - 1):
        total = total + square_z[k]
    square_own[...] = total
    square_r[chip] = total
    over_chips(lambda d, p: send(square_own, square_r.at[chip], 9, p, c))

    take(right.at[pl.ds(0, ys - 1)], recv_sem.at[8])
    block = pl.ds(core * half + x * ys, ys)
    for d in range(1, xs):
        to = lax.rem(x + d, xs)
        send(right.at[block], right.at[block], 10, (y * xs + to) * 2 + core, c)
    take(right.at[pl.ds(0, (xs - 1) * ys)], recv_sem.at[10])
    block = pl.ds(core * half, half)
    send(right.at[block], right.at[block], 11, partner, c)

    take(square_r.at[pl.ds(0, half - 1)], recv_sem.at[9])
    total = square_r[0]
    for k in range(1, half):
        total = total + square_r[k]
    square_half[...] = total
    send(square_half, square_core, 14, partner, c)
    take(square_core, recv_sem.at[14])
    total = total + square_core[...]
    scale_out[...] = jnp.sqrt(total / (ff * zs) + epsilon)
    take(right.at[pl.ds(0, half)], recv_sem.at[11])
    right_out[...] = right[...]

    drain(15)


def finish_kernel(factor, weight, gradient, momentum, ortho, right, scale, weight_out, momentum_out, basis_out):
    cols = weight.shape[1]
    col_scale = scale[...]
    basis = right[...].astype(F32).reshape(cols, 256) / col_scale
    basis_low = basis.astype(BF16)
    basis_out[...] = basis_low.T
    rows = ortho[...]
    scaled = (rows.astype(F32) * col_scale).astype(BF16)
    dims = (((1,), (1,)), ((), ()))
    correction = lax.dot_general(scaled, basis_low, dims, preferred_element_type=F32)
    change = lax.dot_general(rows, basis_low, dims, preferred_element_type=F32)
    buffer = momentum[...] + gradient[...].astype(F32)
    momentum_out[...] = buffer - (1.0 - momentum_decay) * correction
    weight_out[...] = (weight[...].astype(F32) - factor * change).astype(BF16)


def per_device(sizes, dims, weight, gradient, momentum, old_basis):
    ys, xs, zs, ff = sizes
    rows, half, cut, lines = ys * xs * 2, ys * xs, ff // (ys * xs * 2), 128 // zs
    each = 32 // half
    anywhere = pl.BlockSpec(memory_space=pl.ANY)
    inside = pl.BlockSpec(memory_space=pltpu.VMEM)
    ortho, right, scale = pl.pallas_call(
        functools.partial(exchange_kernel, sizes),
        out_shape=(
            jax.ShapeDtypeStruct((128, 256), BF16),
            jax.ShapeDtypeStruct((rows, cut, 256), BF16),
            jax.ShapeDtypeStruct((1, 256), F32),
        ),
        in_specs=[anywhere] * 3,
        out_specs=(inside, inside, inside),
        scratch_shapes=[
            pltpu.VMEM((128, ff), BF16),
            pltpu.VMEM((128, ff), F32),
            pltpu.VMEM((256, ff), BF16),
            pltpu.VMEM((128, ff), BF16),
            pltpu.VMEM((zs, lines, 256), F32),
            pltpu.VMEM((zs - 1, lines, 256), F32),
            pltpu.VMEM((zs, lines, 256), F32),
            pltpu.VMEM((rows, each, 8, 128), F32),
            pltpu.VMEM((half - 1, each, 8, 128), F32),
            pltpu.VMEM((each, 8, 128), F32),
            pltpu.VMEM((rows, each, 8, 128), F32),
            pltpu.VMEM((256, 256), F32),
            pltpu.VMEM((rows, cut, 256), F32),
            pltpu.VMEM((half, cut, 256), F32),
            pltpu.VMEM((half, cut, 256), F32),
            pltpu.VMEM((xs - 1, ys, cut, 256), F32),
            pltpu.VMEM((ys, cut, 256), F32),
            pltpu.VMEM((ys - 1, cut, 256), F32),
            pltpu.VMEM((rows, cut, 256), BF16),
            pltpu.VMEM((1, 256), F32),
            pltpu.VMEM((zs - 1, 1, 256), F32),
            pltpu.VMEM((1, 256), F32),
            pltpu.VMEM((half, 1, 256), F32),
            pltpu.VMEM((1, 256), F32),
            pltpu.VMEM((1, 256), F32),
            pltpu.VMEM((half, each, 8, 128), F32),
            pltpu.VMEM((half, each, 8, 128), F32),
            pltpu.SemaphoreType.DMA((3,)),
            pltpu.SemaphoreType.DMA((15,)),
            pltpu.SemaphoreType.DMA((15,)),
        ],
        compiler_params=pltpu.CompilerParams(
            collective_id=0, has_side_effects=True, vmem_limit_bytes=VMEM
        ),
    )(gradient, momentum, old_basis)
    total_rows, _ = dims
    factor = step_rate * math.sqrt(total_rows / 256)
    steps = 2
    wide = ff // steps
    strip = lambda n: pl.BlockSpec((n, wide), lambda i: (0, i))
    return pl.pallas_call(
        functools.partial(finish_kernel, factor),
        grid=(steps,),
        out_shape=(
            jax.ShapeDtypeStruct((128, ff), BF16),
            jax.ShapeDtypeStruct((128, ff), F32),
            jax.ShapeDtypeStruct((256, ff), BF16),
        ),
        in_specs=[
            strip(128),
            strip(128),
            strip(128),
            pl.BlockSpec((128, 256), lambda i: (0, 0)),
            pl.BlockSpec((rows // steps, cut, 256), lambda i: (i, 0, 0)),
            pl.BlockSpec((1, 256), lambda i: (0, 0)),
        ],
        out_specs=(strip(128), strip(128), strip(256)),
        compiler_params=pltpu.CompilerParams(vmem_limit_bytes=VMEM),
    )(weight, gradient, momentum, ortho, right, scale)


def solution(mesh, xs=4):
    rows, zs = mesh.shape["row"], mesh.shape["col"]
    sizes = (rows // (2 * xs), xs, zs, 1536)
    return jax.shard_map(
        functools.partial(per_device, sizes, (128 * rows, 1536 * zs)),
        mesh=mesh,
        in_specs=(P("row", "col"), P("row", "col"), P("row", "col"), P(None, "col")),
        out_specs=(P("row", "col"), P("row", "col"), P(None, "col")),
        check_vma=False,
    )
```

```python
import functools
import math

import jax
import jax.numpy as jnp
from jax import lax
from jax.experimental import pallas as pl
from jax.experimental.pallas import tpu as pltpu
from jax.sharding import PartitionSpec as P

epsilon = 1e-06
momentum_decay = 0.6
step_rate = 0.5

F32 = jnp.float32
BF16 = jnp.bfloat16
HI = lax.Precision.HIGHEST
MESH = pl.DeviceIdType.MESH
GROUP = 32
VMEM = 67043328


def nt(a, b):
    return lax.dot_general(a, b, (((1,), (1,)), ((), ())), precision=HI, preferred_element_type=F32)


def parts(a):
    high = a.astype(BF16)
    rest = a - high.astype(F32)
    middle = rest.astype(BF16)
    return high, middle, (rest - middle.astype(F32)).astype(BF16)


def tn6(a, b):
    ah, am, al = parts(a)
    bh, bm, bl = parts(b)
    left = jnp.concatenate([al, am, ah, am, ah, ah], axis=0)
    right = jnp.concatenate([bh, bm, bl, bh, bm, bh], axis=0)
    return lax.dot_general(left, right, (((0,), (0,)), ((), ())), preferred_element_type=F32)


def spread(v, i):
    return jnp.broadcast_to(v[i : i + 1, :], (8, 128))


def fill(v, j):
    return jnp.broadcast_to(v[:, j : j + 1], (8, 128))


def tree(terms):
    terms = list(terms)
    while len(terms) > 1:
        pairs = [a + b for a, b in zip(terms[::2], terms[1::2])]
        terms = pairs + terms[len(pairs) * 2 :]
    return terms[0]


def small_inverse(p0):
    cols = [fill(p0, j) for j in range(8)]
    e = {(i, j): spread(cols[j], i) for j in range(8) for i in range(j, 8)}
    low, inv = {}, {}
    for j in range(8):
        r = lax.rsqrt(e[j, j])
        inv[j, j] = r
        for i in range(j + 1, 8):
            low[i, j] = e[i, j] * r
        for k in range(j + 1, 8):
            for i in range(k, 8):
                e[i, k] = e[i, k] - low[i, j] * low[k, j]
    for i in range(8):
        for j in range(i):
            inv[i, j] = -inv[i, i] * tree(low[i, k] * inv[k, j] for k in range(j, i))
    return inv


def panel_step(t, panels, group):
    lane = lax.broadcasted_iota(jnp.int32, (8, 128), 1)
    sub = lax.broadcasted_iota(jnp.int32, (8, 128), 0)
    p = panels[0]
    p0, p1 = p[:, :128], p[:, 128:]
    inv = small_inverse(p0)
    a0 = jnp.where(lane < 8, (lane == sub).astype(F32), p0)
    columns = []
    for j in range(8):
        col = jnp.zeros((8, 128), F32)
        for i in range(j, 8):
            col = jnp.where(sub == i, inv[i, j], col)
        columns.append(col)
    q0 = tree(columns[j] * spread(a0, j) for j in range(8))
    q1 = tree(columns[j] * spread(p1, j) for j in range(8))
    r0 = [spread(q0, k) for k in range(8)]
    r1 = [spread(q1, k) for k in range(8)]
    out = []
    for s in range(1, group):
        b0, b1 = panels[s][:, :128], panels[s][:, 128:]
        live = t + s < group
        cols = [jnp.where(live, fill(b0, j), 0.0) for j in range(8)]
        b0 = jnp.where(jnp.logical_and(lane < 8, live), 0.0, b0)
        ms = [tree(cols[j] * inv[k, j] for j in range(k + 1)) for k in range(8)]
        b0 = b0 - tree(ms[k] * r0[k] for k in range(8))
        b1 = b1 - tree(ms[k] * r1[k] for k in range(8))
        out.append(jnp.concatenate([b0, b1], axis=1))
    out.append(jnp.concatenate([q0, q1], axis=1))
    return tuple(pltpu.roll(v, 248, 1) for v in out)


def inverse_factor(work, size, rows, midway):
    group = rows // 8
    for ob in range(size // rows):
        lo = ob * rows
        if 2 * lo == size:
            midway()
        panels = tuple(work[lo + 8 * i : lo + 8 * i + 8, :] for i in range(group))
        panels = lax.fori_loop(0, group, lambda t, ps: panel_step(t, ps, group), panels)
        q = jnp.concatenate(panels, axis=0)
        rest = size - lo - rows
        lane = lax.broadcasted_iota(jnp.int32, (rows, size), 1)
        row = lax.broadcasted_iota(jnp.int32, (rows, size), 0)
        own = jnp.where(jnp.logical_or(lane < rest, lane > row + (size - rows)), 0.0, q)
        if ob:
            work[:lo, :] = pltpu.roll(work[:lo, :], size - rows, 1)
        work[lo : lo + rows, :] = own
        if rest:
            lane = lax.broadcasted_iota(jnp.int32, (rest, size), 1)
            old = jnp.where(lane < rows, 0.0, work[lo + rows :, :])
            both = jnp.where(lax.broadcasted_iota(jnp.int32, (rows, size), 1) < rest, q, own)
            work[lo + rows :, :] = pltpu.roll(old, size - rows, 1) - tn6(q[:, :rest], both)
def far_first(k, n):
    h = (k + 1) // 2
    return n // 2 + h * (1 - 2 * (k % 2))


def take(ref, sem):
    pltpu.make_async_copy(ref, ref, sem).wait()


def exchange_kernel(
    sizes,
    gradient,
    momentum,
    basis,
    ortho_out,
    right_out,
    scale_out,
    grad_v,
    mom_v,
    basis_v,
    low,
    part,
    z_in,
    left,
    gram,
    gram_in,
    gram_own,
    gram_all,
    work,
    wide,
    core_in,
    core_sum,
    x_in,
    x_sum,
    y_in,
    right,
    square,
    square_z,
    square_own,
    square_r,
    square_half,
    square_core,
    gram_core,
    gram_pair,
    load_sem,
    send_sem,
    recv_sem,
):
    ys, xs, zs, ff = sizes
    rows = ys * xs * 2
    half = ys * xs
    rank = 256
    r = lax.axis_index("row")
    c = lax.axis_index("col")
    core = lax.rem(r, 2)
    x = lax.rem(r // 2, xs)
    y = r // (2 * xs)
    owner = core * half + x * ys + y
    chip = r // 2
    partner = r + 1 - 2 * core

    loads = [
        pltpu.make_async_copy(gradient, grad_v, load_sem.at[0]),
        pltpu.make_async_copy(momentum, mom_v, load_sem.at[1]),
        pltpu.make_async_copy(basis, basis_v, load_sem.at[2]),
    ]
    for copy in loads:
        copy.start()

    def drain(upto):
        sent = [
            z_in, z_in, gram_core, core_in, gram_in, x_in, y_in, square_z,
            right.at[pl.ds(0, ys - 1)], square_r.at[pl.ds(0, half - 1)],
            right.at[pl.ds(0, (xs - 1) * ys)], right.at[pl.ds(0, half)],
            gram_in, gram_core, square_core,
        ]
        for phase in range(upto):
            take(sent[phase], send_sem.at[phase])

    def send(src, dst, phase, row, col):
        pltpu.make_async_remote_copy(
            src_ref=src,
            dst_ref=dst,
            send_sem=send_sem.at[phase],
            recv_sem=recv_sem.at[phase],
            device_id=(row, col),
            device_id_type=MESH,
        ).start()

    def each_chip(k, fn):
        d = far_first(k, half)
        fn(d, 2 * lax.rem(chip + d, half) + core)

    def each_col(k, fn):
        d = far_first(k, zs)
        fn(d, lax.rem(c + d, zs))

    def over_chips(fn):
        lax.fori_loop(0, half - 1, lambda k, _: (each_chip(k, fn), 0)[1], 0)

    def over_cols(fn):
        lax.fori_loop(0, zs - 1, lambda k, _: (each_col(k, fn), 0)[1], 0)

    barrier = pltpu.get_barrier_semaphore()
    over_cols(lambda d, p: pl.semaphore_signal(barrier, inc=1, device_id=(r, p), device_id_type=MESH))
    over_chips(lambda d, p: pl.semaphore_signal(barrier, inc=1, device_id=(p, c), device_id_type=MESH))
    pl.semaphore_signal(barrier, inc=1, device_id=(partner, c), device_id_type=MESH)

    for copy in loads:
        copy.wait()
    low[...] = (mom_v[...] + grad_v[...].astype(F32)).astype(BF16)
    local = lax.dot_general(
        low[...], basis_v[...], (((1,), (1,)), ((), ())), preferred_element_type=F32
    )
    part[...] = local.reshape(part.shape)
    pl.semaphore_wait(barrier, half + zs - 1)

    over_cols(lambda d, p: send(part.at[p], z_in.at[d - 1], 0, r, p))
    mine = part[c]
    take(z_in, recv_sem.at[0])
    for k in range(zs - 1):
        mine = mine + z_in[k]
    left[c] = mine
    over_cols(lambda d, p: send(left.at[c], left.at[c], 1, r, p))
    take(z_in, recv_sem.at[1])

    left_rows = left[...].reshape(128, rank)
    whole = tn6(left_rows, left_rows)
    each = 32 // half
    for h in range(2):
        gram[h * half : (h + 1) * half] = whole[:, h * 128 : (h + 1) * 128].reshape(half, each, 8, 128)
    send(gram.at[pl.ds((1 - core) * half, half)], gram_core, 2, partner, c)

    take(gram_core, recv_sem.at[2])
    gram_pair[...] = gram_core[...] + gram[pl.ds(core * half, half)]
    over_chips(lambda d, p: send(gram_pair.at[p // 2], gram_in.at[d - 1], 12, p, c))

    high = left_rows.astype(BF16)
    rest = left_rows - high.astype(F32)
    middle = rest.astype(BF16)
    lowest = (rest - middle.astype(F32)).astype(BF16)
    count = rows // 4
    for q in range(4):
        cols = low[:, q * (ff // 4) : (q + 1) * (ff // 4)]
        block = sum(
            lax.dot_general(cols, t, (((0,), (0,)), ((), ())), preferred_element_type=F32)
            for t in (lowest, middle, high)
        )
        wide[q * count : (q + 1) * count] = block.reshape(count, ff // rows, rank)
    send(wide.at[pl.ds((1 - core) * half, half)], core_in, 3, partner, c)

    take(gram_in, recv_sem.at[12])
    own = gram_pair[chip]
    for k in range(half - 1):
        own = own + gram_in[k]
    gram_own[...] = own
    mine = core * half + chip
    gram_all[mine] = own
    over_chips(lambda d, p: send(gram_own, gram_all.at[mine], 4, p, c))

    take(core_in, recv_sem.at[3])
    core_sum[...] = core_in[...] + wide[pl.ds(core * half, half)]
    for d in range(1, xs):
        to = lax.rem(x + d, xs)
        send(core_sum.at[pl.ds(to * ys, ys)], x_in.at[d - 1], 5, (y * xs + to) * 2 + core, c)

    def middle_of_factor():
        take(x_in, recv_sem.at[5])
        total = core_sum[pl.ds(x * ys, ys)]
        for k in range(xs - 1):
            total = total + x_in[k]
        x_sum[...] = total

        def step(k, _):
            d = far_first(k, ys)
            to = lax.rem(y + d, ys)
            send(x_sum.at[to], y_in.at[d - 1], 6, (to * xs + x) * 2 + core, c)
            return 0

        lax.fori_loop(0, ys - 1, step, 0)

    take(gram_in, recv_sem.at[4])
    block = pl.ds(core * half, half)
    send(gram_all.at[block], gram_all.at[block], 13, partner, c)
    take(gram_core, recv_sem.at[13])
    for h in range(2):
        work[:, h * 128 : (h + 1) * 128] = gram_all[h * half : (h + 1) * half].reshape(rank, 128)
    inverse_factor(work, rank, GROUP, middle_of_factor)

    take(y_in, recv_sem.at[6])
    slice_sum = x_sum[y]
    for k in range(ys - 1):
        slice_sum = slice_sum + y_in[k]
    inverse = work[...]
    mine = nt(slice_sum, inverse)
    right[owner] = mine.astype(BF16)
    square[...] = jnp.sum(mine * mine, axis=0, keepdims=True)
    over_cols(lambda d, p: send(square, square_z.at[d - 1], 7, r, p))

    def step(k, _):
        to = lax.rem(y + far_first(k, ys), ys)
        send(right.at[owner], right.at[owner], 8, (to * xs + x) * 2 + core, c)
        return 0

    lax.fori_loop(0, ys - 1, step, 0)

    ortho_out[...] = nt(left_rows, inverse).astype(BF16)

    take(right.at[pl.ds(0, ys - 1)], recv_sem.at[8])
    block = pl.ds(core * half + x * ys, ys)
    for d in range(1, xs):
        to = lax.rem(x + d, xs)
        send(right.at[block], right.at[block], 10, (y * xs + to) * 2 + core, c)

    take(square_z, recv_sem.at[7])
    total = square[...]
    for k in range(zs - 1):
        total = total + square_z[k]
    square_own[...] = total
    square_r[chip] = total
    over_chips(lambda d, p: send(square_own, square_r.at[chip], 9, p, c))

    take(right.at[pl.ds(0, (xs - 1) * ys)], recv_sem.at[10])
    block = pl.ds(core * half, half)
    send(right.at[block], right.at[block], 11, partner, c)

    take(square_r.at[pl.ds(0, half - 1)], recv_sem.at[9])
    total = square_r[0]
    for k in range(1, half):
        total = total + square_r[k]
    square_half[...] = total
    send(square_half, square_core, 14, partner, c)
    take(square_core, recv_sem.at[14])
    total = total + square_core[...]
    scale_out[...] = jnp.sqrt(total / (ff * zs) + epsilon)
    take(right.at[pl.ds(0, half)], recv_sem.at[11])
    right_out[...] = right[...]

    drain(15)


def finish_kernel(factor, weight, gradient, momentum, ortho, right, scale, weight_out, momentum_out, basis_out):
    cols = weight.shape[1]
    col_scale = scale[...]
    basis = right[...].astype(F32).reshape(cols, 256) / col_scale
    basis_low = basis.astype(BF16)
    basis_out[...] = basis_low.T
    rows = ortho[...]
    scaled = (rows.astype(F32) * col_scale).astype(BF16)
    dims = (((1,), (1,)), ((), ()))
    correction = lax.dot_general(scaled, basis_low, dims, preferred_element_type=F32)
    change = lax.dot_general(rows, basis_low, dims, preferred_element_type=F32)
    buffer = momentum[...] + gradient[...].astype(F32)
    momentum_out[...] = buffer - (1.0 - momentum_decay) * correction
    weight_out[...] = (weight[...].astype(F32) - factor * change).astype(BF16)


def per_device(sizes, dims, weight, gradient, momentum, old_basis):
    ys, xs, zs, ff = sizes
    rows, half, cut, lines = ys * xs * 2, ys * xs, ff // (ys * xs * 2), 128 // zs
    each = 32 // half
    anywhere = pl.BlockSpec(memory_space=pl.ANY)
    inside = pl.BlockSpec(memory_space=pltpu.VMEM)
    ortho, right, scale = pl.pallas_call(
        functools.partial(exchange_kernel, sizes),
        out_shape=(
            jax.ShapeDtypeStruct((128, 256), BF16),
            jax.ShapeDtypeStruct((rows, cut, 256), BF16),
            jax.ShapeDtypeStruct((1, 256), F32),
        ),
        in_specs=[anywhere] * 3,
        out_specs=(inside, inside, inside),
        scratch_shapes=[
            pltpu.VMEM((128, ff), BF16),
            pltpu.VMEM((128, ff), F32),
            pltpu.VMEM((256, ff), BF16),
            pltpu.VMEM((128, ff), BF16),
            pltpu.VMEM((zs, lines, 256), F32),
            pltpu.VMEM((zs - 1, lines, 256), F32),
            pltpu.VMEM((zs, lines, 256), F32),
            pltpu.VMEM((rows, each, 8, 128), F32),
            pltpu.VMEM((half - 1, each, 8, 128), F32),
            pltpu.VMEM((each, 8, 128), F32),
            pltpu.VMEM((rows, each, 8, 128), F32),
            pltpu.VMEM((256, 256), F32),
            pltpu.VMEM((rows, cut, 256), F32),
            pltpu.VMEM((half, cut, 256), F32),
            pltpu.VMEM((half, cut, 256), F32),
            pltpu.VMEM((xs - 1, ys, cut, 256), F32),
            pltpu.VMEM((ys, cut, 256), F32),
            pltpu.VMEM((ys - 1, cut, 256), F32),
            pltpu.VMEM((rows, cut, 256), BF16),
            pltpu.VMEM((1, 256), F32),
            pltpu.VMEM((zs - 1, 1, 256), F32),
            pltpu.VMEM((1, 256), F32),
            pltpu.VMEM((half, 1, 256), F32),
            pltpu.VMEM((1, 256), F32),
            pltpu.VMEM((1, 256), F32),
            pltpu.VMEM((half, each, 8, 128), F32),
            pltpu.VMEM((half, each, 8, 128), F32),
            pltpu.SemaphoreType.DMA((3,)),
            pltpu.SemaphoreType.DMA((15,)),
            pltpu.SemaphoreType.DMA((15,)),
        ],
        compiler_params=pltpu.CompilerParams(
            collective_id=0, has_side_effects=True, vmem_limit_bytes=VMEM
        ),
    )(gradient, momentum, old_basis)
    total_rows, _ = dims
    factor = step_rate * math.sqrt(total_rows / 256)
    steps = 2
    wide = ff // steps
    strip = lambda n: pl.BlockSpec((n, wide), lambda i: (0, i))
    return pl.pallas_call(
        functools.partial(finish_kernel, factor),
        grid=(steps,),
        out_shape=(
            jax.ShapeDtypeStruct((128, ff), BF16),
            jax.ShapeDtypeStruct((128, ff), F32),
            jax.ShapeDtypeStruct((256, ff), BF16),
        ),
        in_specs=[
            strip(128),
            strip(128),
            strip(128),
            pl.BlockSpec((128, 256), lambda i: (0, 0)),
            pl.BlockSpec((rows // steps, cut, 256), lambda i: (i, 0, 0)),
            pl.BlockSpec((1, 256), lambda i: (0, 0)),
        ],
        out_specs=(strip(128), strip(128), strip(256)),
        compiler_params=pltpu.CompilerParams(vmem_limit_bytes=VMEM),
    )(weight, gradient, momentum, ortho, right, scale)


def solution(mesh, xs=4):
    rows, zs = mesh.shape["row"], mesh.shape["col"]
    sizes = (rows // (2 * xs), xs, zs, 1536)
    return jax.shard_map(
        functools.partial(per_device, sizes, (128 * rows, 1536 * zs)),
        mesh=mesh,
        in_specs=(P("row", "col"), P("row", "col"), P("row", "col"), P(None, "col")),
        out_specs=(P("row", "col"), P("row", "col"), P(None, "col")),
        check_vma=False,
    )
```

```python
import functools
import math

import jax
import jax.numpy as jnp
from jax import lax
from jax.experimental import pallas as pl
from jax.experimental.pallas import tpu as pltpu
from jax.sharding import PartitionSpec as P

epsilon = 1e-06
momentum_decay = 0.6
step_rate = 0.5

F32 = jnp.float32
BF16 = jnp.bfloat16
HI = lax.Precision.HIGHEST
MESH = pl.DeviceIdType.MESH
GROUP = 32
VMEM = 67043328


def nt(a, b):
    return lax.dot_general(a, b, (((1,), (1,)), ((), ())), precision=HI, preferred_element_type=F32)


def parts(a):
    high = a.astype(BF16)
    rest = a - high.astype(F32)
    middle = rest.astype(BF16)
    return high, middle, (rest - middle.astype(F32)).astype(BF16)


def tn6(a, b):
    ah, am, al = parts(a)
    bh, bm, bl = parts(b)
    left = jnp.concatenate([al, am, ah, am, ah, ah], axis=0)
    right = jnp.concatenate([bh, bm, bl, bh, bm, bh], axis=0)
    return lax.dot_general(left, right, (((0,), (0,)), ((), ())), preferred_element_type=F32)


def spread(v, i):
    return jnp.broadcast_to(v[i : i + 1, :], (8, 128))


def fill(v, j):
    return jnp.broadcast_to(v[:, j : j + 1], (8, 128))


def tree(terms):
    terms = list(terms)
    while len(terms) > 1:
        pairs = [a + b for a, b in zip(terms[::2], terms[1::2])]
        terms = pairs + terms[len(pairs) * 2 :]
    return terms[0]


def small_inverse(p0):
    cols = [fill(p0, j) for j in range(8)]
    e = {(i, j): spread(cols[j], i) for j in range(8) for i in range(j, 8)}
    low, inv = {}, {}
    for j in range(8):
        r = lax.rsqrt(e[j, j])
        inv[j, j] = r
        for i in range(j + 1, 8):
            low[i, j] = e[i, j] * r
        for k in range(j + 1, 8):
            for i in range(k, 8):
                e[i, k] = e[i, k] - low[i, j] * low[k, j]
    for i in range(8):
        for j in range(i):
            inv[i, j] = -inv[i, i] * tree(low[i, k] * inv[k, j] for k in range(j, i))
    return inv


def panel_step(t, panels, group):
    lane = lax.broadcasted_iota(jnp.int32, (8, 128), 1)
    sub = lax.broadcasted_iota(jnp.int32, (8, 128), 0)
    p = panels[0]
    p0, p1 = p[:, :128], p[:, 128:]
    inv = small_inverse(p0)
    a0 = jnp.where(lane < 8, (lane == sub).astype(F32), p0)
    columns = []
    for j in range(8):
        col = jnp.zeros((8, 128), F32)
        for i in range(j, 8):
            col = jnp.where(sub == i, inv[i, j], col)
        columns.append(col)
    q0 = tree(columns[j] * spread(a0, j) for j in range(8))
    q1 = tree(columns[j] * spread(p1, j) for j in range(8))
    r0 = [spread(q0, k) for k in range(8)]
    r1 = [spread(q1, k) for k in range(8)]
    out = []
    for s in range(1, group):
        b0, b1 = panels[s][:, :128], panels[s][:, 128:]
        live = t + s < group
        cols = [jnp.where(live, fill(b0, j), 0.0) for j in range(8)]
        b0 = jnp.where(jnp.logical_and(lane < 8, live), 0.0, b0)
        ms = [tree(cols[j] * inv[k, j] for j in range(k + 1)) for k in range(8)]
        b0 = b0 - tree(ms[k] * r0[k] for k in range(8))
        b1 = b1 - tree(ms[k] * r1[k] for k in range(8))
        out.append(jnp.concatenate([b0, b1], axis=1))
    out.append(jnp.concatenate([q0, q1], axis=1))
    return tuple(pltpu.roll(v, 248, 1) for v in out)


def inverse_factor(work, size, rows, midway):
    group = rows // 8
    for ob in range(size // rows):
        lo = ob * rows
        if 8 * lo == 3 * size:
            midway()
        panels = tuple(work[lo + 8 * i : lo + 8 * i + 8, :] for i in range(group))
        panels = lax.fori_loop(0, group, lambda t, ps: panel_step(t, ps, group), panels)
        q = jnp.concatenate(panels, axis=0)
        rest = size - lo - rows
        lane = lax.broadcasted_iota(jnp.int32, (rows, size), 1)
        row = lax.broadcasted_iota(jnp.int32, (rows, size), 0)
        own = jnp.where(jnp.logical_or(lane < rest, lane > row + (size - rows)), 0.0, q)
        if ob:
            work[:lo, :] = pltpu.roll(work[:lo, :], size - rows, 1)
        work[lo : lo + rows, :] = own
        if rest:
            lane = lax.broadcasted_iota(jnp.int32, (rest, size), 1)
            old = jnp.where(lane < rows, 0.0, work[lo + rows :, :])
            both = jnp.where(lax.broadcasted_iota(jnp.int32, (rows, size), 1) < rest, q, own)
            work[lo + rows :, :] = pltpu.roll(old, size - rows, 1) - tn6(q[:, :rest], both)
def far_first(k, n):
    h = (k + 1) // 2
    return n // 2 + h * (1 - 2 * (k % 2))


def take(ref, sem):
    pltpu.make_async_copy(ref, ref, sem).wait()


def exchange_kernel(
    sizes,
    gradient,
    momentum,
    basis,
    ortho_out,
    right_out,
    scale_out,
    grad_v,
    mom_v,
    basis_v,
    low,
    part,
    z_in,
    left,
    gram,
    gram_in,
    gram_own,
    gram_all,
    work,
    wide,
    core_in,
    core_sum,
    x_in,
    x_sum,
    y_in,
    right,
    square,
    square_z,
    square_own,
    square_r,
    square_half,
    square_core,
    gram_core,
    gram_pair,
    load_sem,
    send_sem,
    recv_sem,
):
    ys, xs, zs, ff = sizes
    rows = ys * xs * 2
    half = ys * xs
    rank = 256
    r = lax.axis_index("row")
    c = lax.axis_index("col")
    core = lax.rem(r, 2)
    x = lax.rem(r // 2, xs)
    y = r // (2 * xs)
    owner = core * half + x * ys + y
    chip = r // 2
    partner = r + 1 - 2 * core

    loads = [
        pltpu.make_async_copy(gradient, grad_v, load_sem.at[0]),
        pltpu.make_async_copy(momentum, mom_v, load_sem.at[1]),
        pltpu.make_async_copy(basis, basis_v, load_sem.at[2]),
    ]
    for copy in loads:
        copy.start()

    def drain(upto):
        sent = [
            z_in, z_in, gram_core, core_in, gram_in, x_in, y_in, square_z,
            right.at[pl.ds(0, ys - 1)], square_r.at[pl.ds(0, half - 1)],
            right.at[pl.ds(0, (xs - 1) * ys)], right.at[pl.ds(0, half)],
            gram_in, gram_core, square_core,
        ]
        for phase in range(upto):
            take(sent[phase], send_sem.at[phase])

    def send(src, dst, phase, row, col):
        pltpu.make_async_remote_copy(
            src_ref=src,
            dst_ref=dst,
            send_sem=send_sem.at[phase],
            recv_sem=recv_sem.at[phase],
            device_id=(row, col),
            device_id_type=MESH,
        ).start()

    def each_chip(k, fn):
        d = far_first(k, half)
        fn(d, 2 * lax.rem(chip + d, half) + core)

    def each_col(k, fn):
        d = far_first(k, zs)
        fn(d, lax.rem(c + d, zs))

    def over_chips(fn):
        lax.fori_loop(0, half - 1, lambda k, _: (each_chip(k, fn), 0)[1], 0)

    def over_cols(fn):
        lax.fori_loop(0, zs - 1, lambda k, _: (each_col(k, fn), 0)[1], 0)

    barrier = pltpu.get_barrier_semaphore()
    over_cols(lambda d, p: pl.semaphore_signal(barrier, inc=1, device_id=(r, p), device_id_type=MESH))
    over_chips(lambda d, p: pl.semaphore_signal(barrier, inc=1, device_id=(p, c), device_id_type=MESH))
    pl.semaphore_signal(barrier, inc=1, device_id=(partner, c), device_id_type=MESH)

    for copy in loads:
        copy.wait()
    low[...] = (mom_v[...] + grad_v[...].astype(F32)).astype(BF16)
    local = lax.dot_general(
        low[...], basis_v[...], (((1,), (1,)), ((), ())), preferred_element_type=F32
    )
    part[...] = local.reshape(part.shape)
    pl.semaphore_wait(barrier, half + zs - 1)

    over_cols(lambda d, p: send(part.at[p], z_in.at[d - 1], 0, r, p))
    mine = part[c]
    take(z_in, recv_sem.at[0])
    for k in range(zs - 1):
        mine = mine + z_in[k]
    left[c] = mine
    over_cols(lambda d, p: send(left.at[c], left.at[c], 1, r, p))
    take(z_in, recv_sem.at[1])

    left_rows = left[...].reshape(128, rank)
    whole = tn6(left_rows, left_rows)
    each = 32 // half
    for h in range(2):
        gram[h * half : (h + 1) * half] = whole[:, h * 128 : (h + 1) * 128].reshape(half, each, 8, 128)
    send(gram.at[pl.ds((1 - core) * half, half)], gram_core, 2, partner, c)

    take(gram_core, recv_sem.at[2])
    gram_pair[...] = gram_core[...] + gram[pl.ds(core * half, half)]
    over_chips(lambda d, p: send(gram_pair.at[p // 2], gram_in.at[d - 1], 12, p, c))

    high = left_rows.astype(BF16)
    rest = left_rows - high.astype(F32)
    middle = rest.astype(BF16)
    lowest = (rest - middle.astype(F32)).astype(BF16)
    count = rows // 4
    for q in range(4):
        cols = low[:, q * (ff // 4) : (q + 1) * (ff // 4)]
        block = sum(
            lax.dot_general(cols, t, (((0,), (0,)), ((), ())), preferred_element_type=F32)
            for t in (lowest, middle, high)
        )
        wide[q * count : (q + 1) * count] = block.reshape(count, ff // rows, rank)
    send(wide.at[pl.ds((1 - core) * half, half)], core_in, 3, partner, c)

    take(gram_in, recv_sem.at[12])
    own = gram_pair[chip]
    for k in range(half - 1):
        own = own + gram_in[k]
    gram_own[...] = own
    mine = core * half + chip
    gram_all[mine] = own
    over_chips(lambda d, p: send(gram_own, gram_all.at[mine], 4, p, c))

    take(core_in, recv_sem.at[3])
    core_sum[...] = core_in[...] + wide[pl.ds(core * half, half)]
    for d in range(1, xs):
        to = lax.rem(x + d, xs)
        send(core_sum.at[pl.ds(to * ys, ys)], x_in.at[d - 1], 5, (y * xs + to) * 2 + core, c)

    def middle_of_factor():
        take(x_in, recv_sem.at[5])
        total = core_sum[pl.ds(x * ys, ys)]
        for k in range(xs - 1):
            total = total + x_in[k]
        x_sum[...] = total

        def step(k, _):
            d = far_first(k, ys)
            to = lax.rem(y + d, ys)
            send(x_sum.at[to], y_in.at[d - 1], 6, (to * xs + x) * 2 + core, c)
            return 0

        lax.fori_loop(0, ys - 1, step, 0)

    take(gram_in, recv_sem.at[4])
    block = pl.ds(core * half, half)
    send(gram_all.at[block], gram_all.at[block], 13, partner, c)
    take(gram_core, recv_sem.at[13])
    for h in range(2):
        work[:, h * 128 : (h + 1) * 128] = gram_all[h * half : (h + 1) * half].reshape(rank, 128)
    inverse_factor(work, rank, GROUP, middle_of_factor)

    take(y_in, recv_sem.at[6])
    slice_sum = x_sum[y]
    for k in range(ys - 1):
        slice_sum = slice_sum + y_in[k]
    inverse = work[...]
    mine = nt(slice_sum, inverse)
    right[owner] = mine.astype(BF16)
    square[...] = jnp.sum(mine * mine, axis=0, keepdims=True)
    over_cols(lambda d, p: send(square, square_z.at[d - 1], 7, r, p))

    def step(k, _):
        to = lax.rem(y + far_first(k, ys), ys)
        send(right.at[owner], right.at[owner], 8, (to * xs + x) * 2 + core, c)
        return 0

    lax.fori_loop(0, ys - 1, step, 0)

    ortho_out[...] = nt(left_rows, inverse).astype(BF16)

    take(right.at[pl.ds(0, ys - 1)], recv_sem.at[8])
    block = pl.ds(core * half + x * ys, ys)
    for d in range(1, xs):
        to = lax.rem(x + d, xs)
        send(right.at[block], right.at[block], 10, (y * xs + to) * 2 + core, c)

    take(square_z, recv_sem.at[7])
    total = square[...]
    for k in range(zs - 1):
        total = total + square_z[k]
    square_own[...] = total
    square_r[chip] = total
    over_chips(lambda d, p: send(square_own, square_r.at[chip], 9, p, c))

    take(right.at[pl.ds(0, (xs - 1) * ys)], recv_sem.at[10])
    block = pl.ds(core * half, half)
    send(right.at[block], right.at[block], 11, partner, c)

    take(square_r.at[pl.ds(0, half - 1)], recv_sem.at[9])
    total = square_r[0]
    for k in range(1, half):
        total = total + square_r[k]
    square_half[...] = total
    send(square_half, square_core, 14, partner, c)
    take(square_core, recv_sem.at[14])
    total = total + square_core[...]
    scale_out[...] = jnp.sqrt(total / (ff * zs) + epsilon)
    take(right.at[pl.ds(0, half)], recv_sem.at[11])
    right_out[...] = right[...]

    drain(15)


def finish_kernel(factor, weight, gradient, momentum, ortho, right, scale, weight_out, momentum_out, basis_out):
    cols = weight.shape[1]
    col_scale = scale[...]
    basis = right[...].astype(F32).reshape(cols, 256) / col_scale
    basis_low = basis.astype(BF16)
    basis_out[...] = basis_low.T
    rows = ortho[...]
    scaled = (rows.astype(F32) * col_scale).astype(BF16)
    dims = (((1,), (1,)), ((), ()))
    correction = lax.dot_general(scaled, basis_low, dims, preferred_element_type=F32)
    change = lax.dot_general(rows, basis_low, dims, preferred_element_type=F32)
    buffer = momentum[...] + gradient[...].astype(F32)
    momentum_out[...] = buffer - (1.0 - momentum_decay) * correction
    weight_out[...] = (weight[...].astype(F32) - factor * change).astype(BF16)


def per_device(sizes, dims, weight, gradient, momentum, old_basis):
    ys, xs, zs, ff = sizes
    rows, half, cut, lines = ys * xs * 2, ys * xs, ff // (ys * xs * 2), 128 // zs
    each = 32 // half
    anywhere = pl.BlockSpec(memory_space=pl.ANY)
    inside = pl.BlockSpec(memory_space=pltpu.VMEM)
    ortho, right, scale = pl.pallas_call(
        functools.partial(exchange_kernel, sizes),
        out_shape=(
            jax.ShapeDtypeStruct((128, 256), BF16),
            jax.ShapeDtypeStruct((rows, cut, 256), BF16),
            jax.ShapeDtypeStruct((1, 256), F32),
        ),
        in_specs=[anywhere] * 3,
        out_specs=(inside, inside, inside),
        scratch_shapes=[
            pltpu.VMEM((128, ff), BF16),
            pltpu.VMEM((128, ff), F32),
            pltpu.VMEM((256, ff), BF16),
            pltpu.VMEM((128, ff), BF16),
            pltpu.VMEM((zs, lines, 256), F32),
            pltpu.VMEM((zs - 1, lines, 256), F32),
            pltpu.VMEM((zs, lines, 256), F32),
            pltpu.VMEM((rows, each, 8, 128), F32),
            pltpu.VMEM((half - 1, each, 8, 128), F32),
            pltpu.VMEM((each, 8, 128), F32),
            pltpu.VMEM((rows, each, 8, 128), F32),
            pltpu.VMEM((256, 256), F32),
            pltpu.VMEM((rows, cut, 256), F32),
            pltpu.VMEM((half, cut, 256), F32),
            pltpu.VMEM((half, cut, 256), F32),
            pltpu.VMEM((xs - 1, ys, cut, 256), F32),
            pltpu.VMEM((ys, cut, 256), F32),
            pltpu.VMEM((ys - 1, cut, 256), F32),
            pltpu.VMEM((rows, cut, 256), BF16),
            pltpu.VMEM((1, 256), F32),
            pltpu.VMEM((zs - 1, 1, 256), F32),
            pltpu.VMEM((1, 256), F32),
            pltpu.VMEM((half, 1, 256), F32),
            pltpu.VMEM((1, 256), F32),
            pltpu.VMEM((1, 256), F32),
            pltpu.VMEM((half, each, 8, 128), F32),
            pltpu.VMEM((half, each, 8, 128), F32),
            pltpu.SemaphoreType.DMA((3,)),
            pltpu.SemaphoreType.DMA((15,)),
            pltpu.SemaphoreType.DMA((15,)),
        ],
        compiler_params=pltpu.CompilerParams(
            collective_id=0, has_side_effects=True, vmem_limit_bytes=VMEM
        ),
    )(gradient, momentum, old_basis)
    total_rows, _ = dims
    factor = step_rate * math.sqrt(total_rows / 256)
    steps = 2
    wide = ff // steps
    strip = lambda n: pl.BlockSpec((n, wide), lambda i: (0, i))
    return pl.pallas_call(
        functools.partial(finish_kernel, factor),
        grid=(steps,),
        out_shape=(
            jax.ShapeDtypeStruct((128, ff), BF16),
            jax.ShapeDtypeStruct((128, ff), F32),
            jax.ShapeDtypeStruct((256, ff), BF16),
        ),
        in_specs=[
            strip(128),
            strip(128),
            strip(128),
            pl.BlockSpec((128, 256), lambda i: (0, 0)),
            pl.BlockSpec((rows // steps, cut, 256), lambda i: (i, 0, 0)),
            pl.BlockSpec((1, 256), lambda i: (0, 0)),
        ],
        out_specs=(strip(128), strip(128), strip(256)),
        compiler_params=pltpu.CompilerParams(vmem_limit_bytes=VMEM),
    )(weight, gradient, momentum, ortho, right, scale)


def solution(mesh, xs=4):
    rows, zs = mesh.shape["row"], mesh.shape["col"]
    sizes = (rows // (2 * xs), xs, zs, 1536)
    return jax.shard_map(
        functools.partial(per_device, sizes, (128 * rows, 1536 * zs)),
        mesh=mesh,
        in_specs=(P("row", "col"), P("row", "col"), P("row", "col"), P(None, "col")),
        out_specs=(P("row", "col"), P("row", "col"), P(None, "col")),
        check_vma=False,
    )
```
